32 devices in a mesh: pair: 8 (over z, x), rows: 4 (over y, core).
Axes of the slice: x: 2, y: 2, z: 4, core: 2. Of those that a mesh axis runs over, the one named last changes fastest.
Arguments:
- matrix: float32 [16384, 2048], P('rows', 'pair')
- plan: int32 [3, 8], P(None, 'pair'), may hold values 0 or 1
Outputs:
- rotated: float32 [16384, 2048], P('rows', 'pair')
- offness: float32 [3], replicated
The draws below stay inside these ranges and needn't reach their ends.
All inputs are finite; a program needn't handle non-finite values. No bound on the sum of `plan` on one device may be relied on, other than what follows from the above.
Results may differ from the reference program's by a relative error of at most 0.00025.
Values sent between devices are 32-bit elements; how exact they have to be, the bound alone decides.
A program may use at most 64 MiB of HBM per device.

```python
import math
import jax
import jax.numpy as jnp
from jax import lax

B = 128
ROUNDS = 3
NROWS_ALL = 16384
NCOLS = 2048
N_PAIR = 8


def draw_matrix(key, part):
    keys = jax.random.split(jax.random.fold_in(key, 11), 4)
    factors = jax.random.normal(keys[1], (NROWS_ALL, 4), jnp.float32)
    loads = 0.7 * jax.random.normal(keys[2], (4, NCOLS), jnp.float32)
    pairs_all = NCOLS // (2 * B)
    column = jnp.arange(NCOLS) // (2 * B)
    grade = column.astype(jnp.float32) / jnp.float32(max(pairs_all - 1, 1))
    jitter = jnp.exp(jax.random.uniform(keys[3], (NCOLS,), jnp.float32, 0.0, math.log(2.0)))
    noise = jax.random.normal(keys[0], (NROWS_ALL, NCOLS), jnp.float32)
    column_scale = jnp.exp(0.5 * grade * math.log(3.0)) * jitter
    mixed = noise + factors[:, 0:1] * loads[0:1, :] + factors[:, 1:2] * loads[1:2, :]
    mixed = mixed + factors[:, 2:3] * loads[2:3, :] + factors[:, 3:4] * loads[3:4, :]
    return mixed * column_scale[None, :]


def touch_ends(entries, rng, smallest, top_value):
    shape = entries.shape
    index_at = [jax.random.randint(jax.random.fold_in(rng, axis), (), 0, shape[axis]) for axis in range(len(shape))]
    entries = entries.at[tuple(index_at)].set(smallest)
    longest = shape.index(max(shape))
    index_at[longest] = (index_at[longest] + 1) % shape[longest]
    return entries.at[tuple(index_at)].set(top_value)


def setup_inputs(seed: int = 0) -> dict:
    key_of = jax.random.split(jax.random.key(seed), 3)
    return {
        "matrix": draw_matrix(jax.random.fold_in(key_of[2], 71), 0),
        "plan": touch_ends((jax.random.randint(key_of[1], (ROUNDS, N_PAIR), 0, 2) < 1).astype(jnp.int32), jax.random.fold_in(key_of[1], 1), 0, 1),
    }


def cayley(gram, mean_sq):
    width = gram.shape[-1]
    weights = jnp.arange(width, dtype=jnp.float32) / jnp.float32(width - 1)
    diagonal = jnp.diagonal(gram, axis1=1, axis2=2)
    denom = diagonal[:, :, None] + diagonal[:, None, :] + mean_sq
    skew = gram * (weights[None, None, :] - weights[None, :, None]) / denom
    eye = jnp.eye(width, dtype=jnp.float32)
    square = jnp.einsum('pij,pjk->pik', skew, skew, precision=lax.Precision.HIGHEST)
    plus = eye[None] + skew
    numer = jnp.einsum('pij,pjk->pik', plus, plus, precision=lax.Precision.HIGHEST)
    return jnp.linalg.solve(eye[None] - square, numer)

def reference(matrix, plan):
    width = 2 * B
    cube = matrix.reshape(NROWS_ALL, N_PAIR, width)
    mean_sq = jnp.sum(matrix * matrix) / NCOLS
    eye = jnp.eye(width, dtype=jnp.float32)
    values = []
    for step in range(ROUNDS):
        gram = jnp.einsum('mpi,mpj->pij', cube, cube, precision=lax.Precision.HIGHEST)
        offdiag = gram * (1.0 - eye)[None]
        values.append(jnp.sqrt(jnp.sum(offdiag * offdiag) / (N_PAIR * width * (width - 1))) / mean_sq)
        rotation = cayley(gram, mean_sq)
        turned = jnp.einsum('mpi,pij->mpj', cube, rotation, precision=lax.Precision.HIGHEST)
        keep_last = (plan[step] == 1)[None, :, None]
        first_half = turned[:, :, :B]
        second_half = turned[:, :, B:]
        kept = jnp.where(keep_last, second_half, first_half)
        moving = jnp.where(keep_last, first_half, second_half)
        cube = jnp.concatenate([kept, jnp.roll(moving, 1, axis=1)], axis=2)
    return (cube.reshape(NROWS_ALL, NCOLS), jnp.stack(values))
```

```python
import functools

import jax
import jax.numpy as jnp
from jax import lax
from jax.experimental import pallas as pl
from jax.experimental.pallas import tpu as pltpu
from jax.sharding import PartitionSpec as P

ROUNDS = 3
CHUNKS = 8
STEPS = 7
MESH = pl.DeviceIdType.MESH
F32 = jnp.float32
BF16 = jnp.bfloat16


def split(x):
    high = x.astype(BF16)
    return high, (x - high.astype(F32)).astype(BF16)


def dot(a, b):
    return jnp.dot(a, b, preferred_element_type=F32)


def tdot(a, b):
    return lax.dot_general(a, b, (((0,), (0,)), ((), ())), preferred_element_type=F32)


def full_dot(a, b):
    return jnp.dot(a, b, precision=lax.Precision.HIGHEST, preferred_element_type=F32)


def full_tdot(a, b):
    return lax.dot_general(
        a, b, (((0,), (0,)), ((), ())), precision=lax.Precision.HIGHEST, preferred_element_type=F32
    )


def total(x):
    return jnp.sum(jnp.sum(x, axis=1, keepdims=True), axis=0, keepdims=True)


def scalings(width):
    spread = sum((i - j) ** 2 for i in range(width) for j in range(width)) / (width - 1) ** 2
    top = 1.0 + spread / 8.0
    first = 2.0 / (1.0 + top)
    err = (top - 1.0) / (top + 1.0)
    out = []
    for _ in range(STEPS):
        scale = 2.0 / (2.0 - err * err)
        out.append(scale)
        err = scale - 1.0
    return first, out


def share(axis, peers, tile_ref, slots, send_sems, recv_sems):
    me = lax.axis_index(axis)

    def copy_to(step):
        to = lax.rem(me + step, peers)
        return pltpu.make_async_remote_copy(
            src_ref=tile_ref,
            dst_ref=slots.at[me],
            send_sem=send_sems.at[step],
            recv_sem=recv_sems.at[step],
            device_id={axis: to},
            device_id_type=MESH,
        )

    def start(step, carry):
        copy_to(step).start()
        return carry

    def finish(step, carry):
        copy_to(step).wait()
        return carry

    lax.fori_loop(1, peers, start, 0)

    def done():
        lax.fori_loop(1, peers, finish, 0)
        slots[me] = tile_ref[...]

        def add(i, acc):
            return acc + slots[i]

        return lax.fori_loop(0, peers, add, jnp.zeros(tile_ref.shape, F32))

    return done


def kernel(
    pairs, groups, x_ref, plan_ref, out_ref, off_ref,
    kb, ab, mov, g_ref, acc, q_hi, q_lo, send0, recv0, sendg, recvg, mass_src, mass_in,
    sq_src, sq_rows, sq_tile, sq_pairs, off_tile, off_pairs,
    load_sem, store_sem, move_send, move_recv, ex_send, ex_recv, mass_send, mass_recv,
    sqr_send, sqr_recv, sqp_send, sqp_recv, off_send, off_recv,
):
    rows_all, width = x_ref.shape
    half = width // 2
    rows = rows_all // CHUNKS
    stages = groups.bit_length() - 1
    pair = lax.axis_index("pair")
    group = lax.axis_index("rows")
    after = lax.rem(pair + 1, pairs)

    def at(c):
        return pl.ds(pl.multiple_of(c * rows, rows), rows)

    def load(c, side):
        dst = ab if side else kb
        return pltpu.make_async_copy(
            x_ref.at[at(c), pl.ds(side * half, half)], dst.at[0, at(c)], load_sem.at[side, c]
        )

    def store(c, side):
        src = ab if side else kb
        return pltpu.make_async_copy(
            src.at[ROUNDS, at(c)], out_ref.at[at(c), pl.ds(side * half, half)], store_sem.at[side, c]
        )

    @pl.loop(0, CHUNKS)
    def _(c):
        load(c, 0).start()
        load(c, 1).start()

    barrier = pltpu.get_barrier_semaphore()

    @pl.loop(1, pairs)
    def _(step):
        pl.semaphore_signal(
            barrier, inc=1, device_id={"pair": lax.rem(pair + step, pairs)}, device_id_type=MESH
        )

    @pl.loop(1, groups)
    def _(step):
        pl.semaphore_signal(
            barrier, inc=1, device_id={"rows": lax.rem(group + step, groups)}, device_id_type=MESH
        )

    sq_src[...] = jnp.zeros_like(sq_src)

    @pl.loop(0, CHUNKS)
    def _(c):
        load(c, 0).wait()
        load(c, 1).wait()
        k = kb[0, at(c)]
        m = ab[0, at(c)]
        sq_src[...] += jnp.sum((k * k + m * m).reshape(rows // 8, 8, half), axis=0)

    pl.semaphore_wait(barrier, pairs - 1 + groups - 1)
    rows_done = share("rows", groups, sq_src, sq_rows, sqr_send, sqr_recv)

    g_ref[...] = jnp.zeros_like(g_ref)
    mass_low = jnp.zeros((width, width), F32)

    def first_gram(c, carry):
        high_high, high_low = carry
        high, low = split(jnp.concatenate([kb[0, at(c)], ab[0, at(c)]], axis=1))
        return high_high + tdot(high, high), high_low + tdot(high, low)

    high_high, high_low = lax.fori_loop(0, CHUNKS, first_gram, (mass_low, mass_low))
    gram = high_high + high_low + high_low.T
    send0[0] = jnp.concatenate([gram[:half], gram[half:, half:]], axis=1)

    def swap(send, recv, step, stage):
        return pltpu.make_async_remote_copy(
            src_ref=send.at[stage],
            dst_ref=recv.at[stage],
            send_sem=ex_send.at[step, stage],
            recv_sem=ex_recv.at[step, stage],
            device_id={"rows": jnp.bitwise_xor(group, 1 << stage)},
            device_id_type=MESH,
        )

    def reduce_rows(send, recv, step):
        for stage in range(stages):
            copy = swap(send, recv, step, stage)
            copy.start()
            copy.wait()
            send[stage + 1] = send[stage] + recv[stage]
        return send[stages]

    first_swap = swap(send0, recv0, 0, 0)
    first_swap.start()
    sq_tile[...] = rows_done()
    pairs_done = share("pair", pairs, sq_tile, sq_pairs, sqp_send, sqp_recv)
    first_swap.wait()
    send0[1] = send0[0] + recv0[0]
    for stage in range(1, stages):
        copy = swap(send0, recv0, 0, stage)
        copy.start()
        copy.wait()
        send0[stage + 1] = send0[stage] + recv0[stage]
    gram = send0[stages]
    g_ref[:half, :] = gram[:, :width]
    g_ref[half:, :half] = gram[:, half:width].T
    g_ref[half:, half:] = gram[:, width:]
    mean_sq = total(pairs_done()) / (width * pairs)

    row_id = lax.broadcasted_iota(jnp.int32, (width, width), 0)
    col_id = lax.broadcasted_iota(jnp.int32, (width, width), 1)
    eye = (row_id == col_id).astype(F32)
    off_tile[...] = jnp.zeros_like(off_tile)
    first_scale, scales = scalings(width)

    def move(r, c):
        return pltpu.make_async_remote_copy(
            src_ref=mov.at[r, at(c)],
            dst_ref=ab.at[r + 1, at(c)],
            send_sem=move_send.at[r, c],
            recv_sem=move_recv.at[r, c],
            device_id={"pair": after},
            device_id_type=MESH,
        )

    def pass_mass(r):
        return pltpu.make_async_remote_copy(
            src_ref=mass_src.at[r],
            dst_ref=mass_in.at[r],
            send_sem=mass_send.at[r],
            recv_sem=mass_recv.at[r],
            device_id={"pair": after},
            device_id_type=MESH,
        )

    @pl.loop(0, ROUNDS)
    def _(r):
        gram = g_ref[...]
        diag = gram * eye
        denom = jnp.sum(diag, axis=1, keepdims=True) + jnp.sum(diag, axis=0, keepdims=True) + mean_sq
        weight = (col_id.astype(F32) - row_id.astype(F32)) * F32(1.0 / (width - 1))
        skew = gram * weight / denom
        square = full_dot(skew, skew)
        resid = eye - F32(first_scale) * (eye - square)
        inverse = F32(first_scale) * (eye + skew)

        def refine(i, carry):
            resid, inverse = carry
            scale = F32(scales[0])
            for j in range(1, STEPS - 1):
                scale = jnp.where(i == j, F32(scales[j]), scale)
            inverse = scale * (inverse + full_dot(inverse, resid))
            resid = scale * full_dot(resid, resid) + (1.0 - scale) * eye
            return resid, inverse

        resid, inverse = lax.fori_loop(0, STEPS - 1, refine, (resid, inverse))
        inverse = F32(scales[STEPS - 1]) * (inverse + full_dot(inverse, resid))
        wrong = eye - (inverse - full_dot(skew, inverse))
        inverse = inverse + full_dot(inverse, wrong)
        rotation = 2.0 * inverse - eye
        flag = jnp.full((width, width), plan_ref[r, 0], jnp.int32)
        turned = jnp.concatenate([rotation[:, half:], rotation[:, :half]], axis=1)
        rotation = jnp.where(flag == 1, turned, rotation)
        high, low = split(rotation)
        q_hi[...] = high
        q_lo[...] = low

        @pl.loop(0, CHUNKS)
        def _(c):
            high, low = split(jnp.concatenate([kb[r, at(c)], ab[r, at(c)]], axis=1))
            y = dot(high, q_hi[...]) + (dot(high, q_lo[...]) + dot(low, q_hi[...]))
            mov[r, at(c)] = y[:, half:]
            move(r, c).start()
            kb[r + 1, at(c)] = y[:, :half]

        off = gram * (1.0 - eye)
        tile_row = lax.broadcasted_iota(jnp.int32, off_tile.shape, 0)
        off_tile[...] = jnp.where(tile_row == r, total(off * off), off_tile[...])

        @pl.when(r < ROUNDS - 1)
        def _():
            mass = full_tdot(rotation, full_dot(gram, rotation))
            mass_src[r] = mass[half:, half:]
            pass_mass(r).start()
            g_ref[:half, :half] = mass[:half, :half]
            acc[...] = jnp.zeros_like(acc)

            @pl.loop(0, CHUNKS)
            def _(c):
                k_high, k_low = split(kb[r + 1, at(c)])
                move(r, c).wait()
                m_high, m_low = split(ab[r + 1, at(c)])
                acc[...] += tdot(k_high, m_high) + (tdot(k_high, m_low) + tdot(k_low, m_high))

            sendg[r, 0] = acc[...]
            cross = reduce_rows(sendg.at[r], recvg.at[r], r + 1)
            pass_mass(r).wait()
            g_ref[:half, half:] = cross
            g_ref[half:, :half] = cross.T
            g_ref[half:, half:] = mass_in[r]

    off_done = share("pair", pairs, off_tile, off_pairs, off_send, off_recv)

    @pl.loop(0, CHUNKS)
    def _(c):
        store(c, 0).start()

    off_ref[...] = jnp.sqrt(off_done() / (pairs * width * (width - 1))) / mean_sq

    @pl.loop(0, CHUNKS)
    def _(c):
        move(ROUNDS - 1, c).wait()
        store(c, 1).start()

    @pl.loop(0, CHUNKS)
    def _(c):
        store(c, 0).wait()
        store(c, 1).wait()


def local(matrix, plan):
    rows, width = matrix.shape
    half = width // 2
    pairs = lax.axis_size("pair")
    groups = lax.axis_size("rows")
    if groups & (groups - 1) or rows % (CHUNKS * 8):
        raise ValueError("sizes")
    stages = groups.bit_length() - 1
    dma = pltpu.SemaphoreType.DMA
    tile = (8, 128)
    rotated, off = pl.pallas_call(
        functools.partial(kernel, pairs, groups),
        out_shape=(
            jax.ShapeDtypeStruct(matrix.shape, F32),
            jax.ShapeDtypeStruct(tile, F32),
        ),
        in_specs=[pl.BlockSpec(memory_space=pl.ANY), pl.BlockSpec(memory_space=pltpu.SMEM)],
        out_specs=(pl.BlockSpec(memory_space=pl.ANY), pl.BlockSpec(memory_space=pltpu.VMEM)),
        scratch_shapes=[
            pltpu.VMEM((ROUNDS + 1, rows, half), F32),
            pltpu.VMEM((ROUNDS + 1, rows, half), F32),
            pltpu.VMEM((ROUNDS, rows, half), F32),
            pltpu.VMEM((width, width), F32),
            pltpu.VMEM((half, half), F32),
            pltpu.VMEM((width, width), BF16),
            pltpu.VMEM((width, width), BF16),
            pltpu.VMEM((stages + 1, half, 3 * half), F32),
            pltpu.VMEM((stages, half, 3 * half), F32),
            pltpu.VMEM((ROUNDS, stages + 1, half, half), F32),
            pltpu.VMEM((ROUNDS, stages, half, half), F32),
            pltpu.VMEM((ROUNDS, half, half), F32),
            pltpu.VMEM((ROUNDS, half, half), F32),
            pltpu.VMEM(tile, F32),
            pltpu.VMEM((groups,) + tile, F32),
            pltpu.VMEM(tile, F32),
            pltpu.VMEM((pairs,) + tile, F32),
            pltpu.VMEM(tile, F32),
            pltpu.VMEM((pairs,) + tile, F32),
            dma((2, CHUNKS)),
            dma((2, CHUNKS)),
            dma((ROUNDS, CHUNKS)),
            dma((ROUNDS, CHUNKS)),
            dma((ROUNDS, stages)),
            dma((ROUNDS, stages)),
            dma((ROUNDS,)),
            dma((ROUNDS,)),
            dma((groups,)),
            dma((groups,)),
            dma((pairs,)),
            dma((pairs,)),
            dma((pairs,)),
            dma((pairs,)),
        ],
        compiler_params=pltpu.CompilerParams(
            collective_id=0, has_side_effects=True, vmem_limit_bytes=50 * 2**20
        ),
    )(matrix, plan)
    return rotated, off[:ROUNDS, 0]


def solution(mesh):
    in_specs = (P("rows", "pair"), P(None, "pair"))
    out_specs = (P("rows", "pair"), P())
    return jax.shard_map(local, mesh=mesh, in_specs=in_specs, out_specs=out_specs, check_vma=False)
```

```python
import functools

import jax
import jax.numpy as jnp
from jax import lax
from jax.experimental import pallas as pl
from jax.experimental.pallas import tpu as pltpu
from jax.sharding import PartitionSpec as P

ROUNDS = 3
CHUNKS = 16
STEPS = 7
MESH = pl.DeviceIdType.MESH
F32 = jnp.float32
BF16 = jnp.bfloat16


def split(x):
    high = x.astype(BF16)
    return high, (x - high.astype(F32)).astype(BF16)


def dot(a, b):
    return jnp.dot(a, b, preferred_element_type=F32)


def tdot(a, b):
    return lax.dot_general(a, b, (((0,), (0,)), ((), ())), preferred_element_type=F32)


def full_dot(a, b):
    return jnp.dot(a, b, precision=lax.Precision.HIGHEST, preferred_element_type=F32)


def wide_dot(a, b):
    a_high, a_low = split(a)
    b_high, b_low = split(b)
    return dot(a_high, b_high) + (dot(a_high, b_low) + dot(a_low, b_high))


def full_tdot(a, b):
    return lax.dot_general(
        a, b, (((0,), (0,)), ((), ())), precision=lax.Precision.HIGHEST, preferred_element_type=F32
    )


def total(x):
    return jnp.sum(jnp.sum(x, axis=1, keepdims=True), axis=0, keepdims=True)


def scalings(width):
    spread = sum((i - j) ** 2 for i in range(width) for j in range(width)) / (width - 1) ** 2
    top = 1.0 + spread / 8.0
    first = 2.0 / (1.0 + top)
    err = (top - 1.0) / (top + 1.0)
    out = []
    for _ in range(STEPS):
        scale = 2.0 / (2.0 - err * err)
        out.append(scale)
        err = scale - 1.0
    return first, out


def share(axis, peers, tile_ref, slots, send_sems, recv_sems):
    me = lax.axis_index(axis)

    def copy_to(step):
        to = lax.rem(me + step, peers)
        return pltpu.make_async_remote_copy(
            src_ref=tile_ref,
            dst_ref=slots.at[me],
            send_sem=send_sems.at[step],
            recv_sem=recv_sems.at[step],
            device_id={axis: to},
            device_id_type=MESH,
        )

    def start(step, carry):
        copy_to(step).start()
        return carry

    def finish(step, carry):
        copy_to(step).wait()
        return carry

    lax.fori_loop(1, peers, start, 0)

    def done():
        lax.fori_loop(1, peers, finish, 0)
        slots[me] = tile_ref[...]

        def add(i, acc):
            return acc + slots[i]

        return lax.fori_loop(0, peers, add, jnp.zeros(tile_ref.shape, F32))

    return done


def kernel(
    pairs, groups, x_ref, plan_ref, out_ref, off_ref,
    kb, ab, mov, g_ref, acc, q_hi, q_lo, send0, recv0, sendg, recvg, mass_src, mass_in,
    sq_src, sq_rows, sq_tile, sq_pairs, off_tile, off_pairs,
    load_sem, store_sem, move_send, move_recv, ex_send, ex_recv, mass_send, mass_recv,
    sqr_send, sqr_recv, sqp_send, sqp_recv, off_send, off_recv,
):
    rows_all, width = x_ref.shape
    half = width // 2
    rows = rows_all // CHUNKS
    stages = groups.bit_length() - 1
    pair = lax.axis_index("pair")
    group = lax.axis_index("rows")
    after = lax.rem(pair + 1, pairs)

    def at(c):
        return pl.ds(pl.multiple_of(c * rows, rows), rows)

    def load(c, side):
        dst = ab if side else kb
        return pltpu.make_async_copy(
            x_ref.at[at(c), pl.ds(side * half, half)], dst.at[0, at(c)], load_sem.at[side, c]
        )

    def store(c, side):
        src = ab if side else kb
        return pltpu.make_async_copy(
            src.at[ROUNDS, at(c)], out_ref.at[at(c), pl.ds(side * half, half)], store_sem.at[side, c]
        )

    @pl.loop(0, CHUNKS)
    def _(c):
        load(c, 0).start()
        load(c, 1).start()

    barrier = pltpu.get_barrier_semaphore()

    @pl.loop(1, pairs)
    def _(step):
        pl.semaphore_signal(
            barrier, inc=1, device_id={"pair": lax.rem(pair + step, pairs)}, device_id_type=MESH
        )

    @pl.loop(1, groups)
    def _(step):
        pl.semaphore_signal(
            barrier, inc=1, device_id={"rows": lax.rem(group + step, groups)}, device_id_type=MESH
        )

    sq_src[...] = jnp.zeros_like(sq_src)

    @pl.loop(0, CHUNKS)
    def _(c):
        load(c, 0).wait()
        load(c, 1).wait()
        k = kb[0, at(c)]
        m = ab[0, at(c)]
        sq_src[...] += jnp.sum((k * k + m * m).reshape(rows // 8, 8, half), axis=0)

    pl.semaphore_wait(barrier, pairs - 1 + groups - 1)
    rows_done = share("rows", groups, sq_src, sq_rows, sqr_send, sqr_recv)

    g_ref[...] = jnp.zeros_like(g_ref)
    mass_low = jnp.zeros((width, width), F32)

    def first_gram(c, carry):
        high_high, high_low = carry
        high, low = split(jnp.concatenate([kb[0, at(c)], ab[0, at(c)]], axis=1))
        return high_high + tdot(high, high), high_low + tdot(high, low)

    high_high, high_low = lax.fori_loop(0, CHUNKS, first_gram, (mass_low, mass_low))
    gram = high_high + high_low + high_low.T
    send0[0] = jnp.concatenate([gram[:half], gram[half:, half:]], axis=1)

    def swap(send, recv, step, stage):
        return pltpu.make_async_remote_copy(
            src_ref=send.at[stage],
            dst_ref=recv.at[stage],
            send_sem=ex_send.at[step, stage],
            recv_sem=ex_recv.at[step, stage],
            device_id={"rows": jnp.bitwise_xor(group, 1 << stage)},
            device_id_type=MESH,
        )

    def reduce_rows(send, recv, step):
        for stage in range(stages):
            copy = swap(send, recv, step, stage)
            copy.start()
            copy.wait()
            send[stage + 1] = send[stage] + recv[stage]
        return send[stages]

    first_swap = swap(send0, recv0, 0, 0)
    first_swap.start()
    sq_tile[...] = rows_done()
    pairs_done = share("pair", pairs, sq_tile, sq_pairs, sqp_send, sqp_recv)
    first_swap.wait()
    send0[1] = send0[0] + recv0[0]
    for stage in range(1, stages):
        copy = swap(send0, recv0, 0, stage)
        copy.start()
        copy.wait()
        send0[stage + 1] = send0[stage] + recv0[stage]
    gram = send0[stages]
    g_ref[:half, :] = gram[:, :width]
    g_ref[half:, :half] = gram[:, half:width].T
    g_ref[half:, half:] = gram[:, width:]
    mean_sq = total(pairs_done()) / (width * pairs)

    row_id = lax.broadcasted_iota(jnp.int32, (width, width), 0)
    col_id = lax.broadcasted_iota(jnp.int32, (width, width), 1)
    eye = (row_id == col_id).astype(F32)
    off_tile[...] = jnp.zeros_like(off_tile)
    first_scale, scales = scalings(width)

    def move(r, c):
        return pltpu.make_async_remote_copy(
            src_ref=mov.at[r, at(c)],
            dst_ref=ab.at[r + 1, at(c)],
            send_sem=move_send.at[r, c],
            recv_sem=move_recv.at[r, c],
            device_id={"pair": after},
            device_id_type=MESH,
        )

    def pass_mass(r):
        return pltpu.make_async_remote_copy(
            src_ref=mass_src.at[r],
            dst_ref=mass_in.at[r],
            send_sem=mass_send.at[r],
            recv_sem=mass_recv.at[r],
            device_id={"pair": after},
            device_id_type=MESH,
        )

    @pl.loop(0, ROUNDS)
    def _(r):
        gram = g_ref[...]
        diag = gram * eye
        denom = jnp.sum(diag, axis=1, keepdims=True) + jnp.sum(diag, axis=0, keepdims=True) + mean_sq
        weight = (col_id.astype(F32) - row_id.astype(F32)) * F32(1.0 / (width - 1))
        skew = gram * weight / denom
        square = wide_dot(skew, skew)
        resid = eye - F32(first_scale) * (eye - square)
        inverse = F32(first_scale) * (eye + skew)

        def refine(i, carry):
            resid, inverse = carry
            scale = F32(scales[0])
            for j in range(1, STEPS - 1):
                scale = jnp.where(i == j, F32(scales[j]), scale)
            inverse = scale * (inverse + wide_dot(inverse, resid))
            resid = scale * wide_dot(resid, resid) + (1.0 - scale) * eye
            return resid, inverse

        resid, inverse = lax.fori_loop(0, STEPS - 1, refine, (resid, inverse))
        inverse = F32(scales[STEPS - 1]) * (inverse + wide_dot(inverse, resid))
        wrong = eye - (inverse - full_dot(skew, inverse))
        inverse = inverse + wide_dot(inverse, wrong)
        rotation = 2.0 * inverse - eye
        flag = jnp.full((width, width), plan_ref[r, 0], jnp.int32)
        turned = jnp.concatenate([rotation[:, half:], rotation[:, :half]], axis=1)
        rotation = jnp.where(flag == 1, turned, rotation)
        high, low = split(rotation)
        q_hi[...] = high
        q_lo[...] = low

        @pl.loop(0, CHUNKS)
        def _(c):
            high, low = split(jnp.concatenate([kb[r, at(c)], ab[r, at(c)]], axis=1))
            y = dot(high, q_hi[...]) + (dot(high, q_lo[...]) + dot(low, q_hi[...]))
            mov[r, at(c)] = y[:, half:]
            move(r, c).start()
            kb[r + 1, at(c)] = y[:, :half]

        off = gram * (1.0 - eye)
        tile_row = lax.broadcasted_iota(jnp.int32, off_tile.shape, 0)
        off_tile[...] = jnp.where(tile_row == r, total(off * off), off_tile[...])

        @pl.when(r < ROUNDS - 1)
        def _():
            mass = full_tdot(rotation, full_dot(gram, rotation))
            mass_src[r] = mass[half:, half:]
            pass_mass(r).start()
            g_ref[:half, :half] = mass[:half, :half]
            acc[...] = jnp.zeros_like(acc)

            @pl.loop(0, CHUNKS)
            def _(c):
                k_high, k_low = split(kb[r + 1, at(c)])
                move(r, c).wait()
                m_high, m_low = split(ab[r + 1, at(c)])
                acc[...] += tdot(k_high, m_high) + (tdot(k_high, m_low) + tdot(k_low, m_high))

            sendg[r, 0] = acc[...]
            cross = reduce_rows(sendg.at[r], recvg.at[r], r + 1)
            pass_mass(r).wait()
            g_ref[:half, half:] = cross
            g_ref[half:, :half] = cross.T
            g_ref[half:, half:] = mass_in[r]

    off_done = share("pair", pairs, off_tile, off_pairs, off_send, off_recv)

    @pl.loop(0, CHUNKS)
    def _(c):
        store(c, 0).start()

    off_ref[...] = jnp.sqrt(off_done() / (pairs * width * (width - 1))) / mean_sq

    @pl.loop(0, CHUNKS)
    def _(c):
        move(ROUNDS - 1, c).wait()
        store(c, 1).start()

    @pl.loop(0, CHUNKS)
    def _(c):
        store(c, 0).wait()
        store(c, 1).wait()


def local(matrix, plan):
    rows, width = matrix.shape
    half = width // 2
    pairs = lax.axis_size("pair")
    groups = lax.axis_size("rows")
    if groups & (groups - 1) or rows % (CHUNKS * 8):
        raise ValueError("sizes")
    stages = groups.bit_length() - 1
    dma = pltpu.SemaphoreType.DMA
    tile = (8, 128)
    rotated, off = pl.pallas_call(
        functools.partial(kernel, pairs, groups),
        out_shape=(
            jax.ShapeDtypeStruct(matrix.shape, F32),
            jax.ShapeDtypeStruct(tile, F32),
        ),
        in_specs=[pl.BlockSpec(memory_space=pl.ANY), pl.BlockSpec(memory_space=pltpu.SMEM)],
        out_specs=(pl.BlockSpec(memory_space=pl.ANY), pl.BlockSpec(memory_space=pltpu.VMEM)),
        scratch_shapes=[
            pltpu.VMEM((ROUNDS + 1, rows, half), F32),
            pltpu.VMEM((ROUNDS + 1, rows, half), F32),
            pltpu.VMEM((ROUNDS, rows, half), F32),
            pltpu.VMEM((width, width), F32),
            pltpu.VMEM((half, half), F32),
            pltpu.VMEM((width, width), BF16),
            pltpu.VMEM((width, width), BF16),
            pltpu.VMEM((stages + 1, half, 3 * half), F32),
            pltpu.VMEM((stages, half, 3 * half), F32),
            pltpu.VMEM((ROUNDS, stages + 1, half, half), F32),
            pltpu.VMEM((ROUNDS, stages, half, half), F32),
            pltpu.VMEM((ROUNDS, half, half), F32),
            pltpu.VMEM((ROUNDS, half, half), F32),
            pltpu.VMEM(tile, F32),
            pltpu.VMEM((groups,) + tile, F32),
            pltpu.VMEM(tile, F32),
            pltpu.VMEM((pairs,) + tile, F32),
            pltpu.VMEM(tile, F32),
            pltpu.VMEM((pairs,) + tile, F32),
            dma((2, CHUNKS)),
            dma((2, CHUNKS)),
            dma((ROUNDS, CHUNKS)),
            dma((ROUNDS, CHUNKS)),
            dma((ROUNDS, stages)),
            dma((ROUNDS, stages)),
            dma((ROUNDS,)),
            dma((ROUNDS,)),
            dma((groups,)),
            dma((groups,)),
            dma((pairs,)),
            dma((pairs,)),
            dma((pairs,)),
            dma((pairs,)),
        ],
        compiler_params=pltpu.CompilerParams(
            collective_id=0, has_side_effects=True, vmem_limit_bytes=50 * 2**20
        ),
    )(matrix, plan)
    return rotated, off[:ROUNDS, 0]


def solution(mesh):
    in_specs = (P("rows", "pair"), P(None, "pair"))
    out_specs = (P("rows", "pair"), P())
    return jax.shard_map(local, mesh=mesh, in_specs=in_specs, out_specs=out_specs, check_vma=False)
```

```python
import functools

import jax
import jax.numpy as jnp
from jax import lax
from jax.experimental import pallas as pl
from jax.experimental.pallas import tpu as pltpu
from jax.sharding import PartitionSpec as P

ROUNDS = 3
CHUNKS = 8
RAW_BLOCKS = 2
STEPS = 7
MESH = pl.DeviceIdType.MESH
F32 = jnp.float32
BF16 = jnp.bfloat16


def split(x):
    high = x.astype(BF16)
    return high, (x - high.astype(F32)).astype(BF16)


def dot(a, b):
    return jnp.dot(a, b, preferred_element_type=F32)


def tdot(a, b):
    return lax.dot_general(a, b, (((0,), (0,)), ((), ())), preferred_element_type=F32)


def full_dot(a, b):
    return jnp.dot(a, b, precision=lax.Precision.HIGHEST, preferred_element_type=F32)


def wide_dot(a, b):
    a_high, a_low = split(a)
    b_high, b_low = split(b)
    return dot(a_high, b_high) + (dot(a_high, b_low) + dot(a_low, b_high))


def full_tdot(a, b):
    return lax.dot_general(
        a, b, (((0,), (0,)), ((), ())), precision=lax.Precision.HIGHEST, preferred_element_type=F32
    )


def total(x):
    return jnp.sum(jnp.sum(x, axis=1, keepdims=True), axis=0, keepdims=True)


def scalings(width):
    spread = sum((i - j) ** 2 for i in range(width) for j in range(width)) / (width - 1) ** 2
    top = 1.0 + spread / 8.0
    first = 2.0 / (1.0 + top)
    err = (top - 1.0) / (top + 1.0)
    out = []
    for _ in range(STEPS):
        scale = 2.0 / (2.0 - err * err)
        out.append(scale)
        err = scale - 1.0
    return first, out


def share(axis, peers, tile_ref, slots, send_sems, recv_sems):
    me = lax.axis_index(axis)

    def copy_to(step):
        to = lax.rem(me + step, peers)
        return pltpu.make_async_remote_copy(
            src_ref=tile_ref,
            dst_ref=slots.at[me],
            send_sem=send_sems.at[step],
            recv_sem=recv_sems.at[step],
            device_id={axis: to},
            device_id_type=MESH,
        )

    def start(step, carry):
        copy_to(step).start()
        return carry

    def finish(step, carry):
        copy_to(step).wait()
        return carry

    lax.fori_loop(1, peers, start, 0)

    def done():
        lax.fori_loop(1, peers, finish, 0)
        slots[me] = tile_ref[...]

        def add(i, acc):
            return acc + slots[i]

        return lax.fori_loop(0, peers, add, jnp.zeros(tile_ref.shape, F32))

    return done


def kernel(
    pairs, groups, x_ref, plan_ref, out_ref, off_ref,
    kb, ab, mov, g_ref, acc, q_hi, q_lo, send0, recv0, sendg, recvg, mass_src, mass_in,
    sq_src, sq_rows, sq_tile, sq_pairs, off_tile, off_pairs, raw_in, q_src, q_in,
    load_sem, store_sem, move_send, move_recv, ex_send, ex_recv, mass_send, mass_recv,
    sqr_send, sqr_recv, sqp_send, sqp_recv, off_send, off_recv,
    raw_send, raw_recv, q_send, q_recv,
):
    rows_all, width = x_ref.shape
    half = width // 2
    raw = raw_in.shape[2]
    rows = (rows_all - raw) // CHUNKS
    load_rows = rows_all // CHUNKS
    raw_rows = raw // RAW_BLOCKS
    stages = groups.bit_length() - 1
    pair = lax.axis_index("pair")
    group = lax.axis_index("rows")
    after = lax.rem(pair + 1, pairs)

    def at(c):
        return pl.ds(pl.multiple_of(raw + c * rows, 16), rows)

    def load_at(c):
        return pl.ds(pl.multiple_of(c * load_rows, load_rows), load_rows)

    def raw_at(c):
        return pl.ds(pl.multiple_of(c * raw_rows, raw_rows), raw_rows)

    def load(c, side):
        dst = ab if side else kb
        return pltpu.make_async_copy(
            x_ref.at[load_at(c), pl.ds(side * half, half)], dst.at[0, load_at(c)], load_sem.at[side, c]
        )

    def store(c, side):
        src = ab if side else kb
        return pltpu.make_async_copy(
            src.at[ROUNDS, at(c)], out_ref.at[at(c), pl.ds(side * half, half)], store_sem.at[side, c]
        )

    def store_raw(side):
        src = ab if side else kb
        where = pl.ds(0, raw)
        return pltpu.make_async_copy(
            src.at[ROUNDS, where], out_ref.at[where, pl.ds(side * half, half)], store_sem.at[side, CHUNKS]
        )

    def pass_raw(r, side):
        src = ab if side else kb
        return pltpu.make_async_remote_copy(
            src_ref=src.at[r, pl.ds(0, raw)],
            dst_ref=raw_in.at[r, side],
            send_sem=raw_send.at[r, side],
            recv_sem=raw_recv.at[r, side],
            device_id={"pair": after},
            device_id_type=MESH,
        )

    def pass_q(r):
        return pltpu.make_async_remote_copy(
            src_ref=q_src.at[r],
            dst_ref=q_in.at[r],
            send_sem=q_send.at[r],
            recv_sem=q_recv.at[r],
            device_id={"pair": after},
            device_id_type=MESH,
        )

    @pl.loop(0, CHUNKS)
    def _(c):
        load(c, 0).start()
        load(c, 1).start()

    barrier = pltpu.get_barrier_semaphore()

    @pl.loop(1, pairs)
    def _(step):
        pl.semaphore_signal(
            barrier, inc=1, device_id={"pair": lax.rem(pair + step, pairs)}, device_id_type=MESH
        )

    @pl.loop(1, groups)
    def _(step):
        pl.semaphore_signal(
            barrier, inc=1, device_id={"rows": lax.rem(group + step, groups)}, device_id_type=MESH
        )

    sq_src[...] = jnp.zeros_like(sq_src)

    @pl.loop(0, CHUNKS)
    def _(c):
        load(c, 0).wait()
        load(c, 1).wait()
        k = kb[0, load_at(c)]
        m = ab[0, load_at(c)]
        sq_src[...] += jnp.sum((k * k + m * m).reshape(load_rows // 8, 8, half), axis=0)

    pl.semaphore_wait(barrier, pairs - 1 + groups - 1)
    pass_raw(0, 0).start()
    pass_raw(0, 1).start()
    rows_done = share("rows", groups, sq_src, sq_rows, sqr_send, sqr_recv)

    g_ref[...] = jnp.zeros_like(g_ref)
    mass_low = jnp.zeros((width, width), F32)

    def first_gram(c, carry):
        high_high, high_low = carry
        high, low = split(jnp.concatenate([kb[0, load_at(c)], ab[0, load_at(c)]], axis=1))
        return high_high + tdot(high, high), high_low + tdot(high, low)

    high_high, high_low = lax.fori_loop(0, CHUNKS, first_gram, (mass_low, mass_low))
    gram = high_high + high_low + high_low.T
    send0[0] = jnp.concatenate([gram[:half], gram[half:, half:]], axis=1)

    def swap(send, recv, step, stage):
        return pltpu.make_async_remote_copy(
            src_ref=send.at[stage],
            dst_ref=recv.at[stage],
            send_sem=ex_send.at[step, stage],
            recv_sem=ex_recv.at[step, stage],
            device_id={"rows": jnp.bitwise_xor(group, 1 << stage)},
            device_id_type=MESH,
        )

    def reduce_rows(send, recv, step):
        for stage in range(stages):
            copy = swap(send, recv, step, stage)
            copy.start()
            copy.wait()
            send[stage + 1] = send[stage] + recv[stage]
        return send[stages]

    first_swap = swap(send0, recv0, 0, 0)
    first_swap.start()
    sq_tile[...] = rows_done()
    pairs_done = share("pair", pairs, sq_tile, sq_pairs, sqp_send, sqp_recv)
    first_swap.wait()
    send0[1] = send0[0] + recv0[0]
    for stage in range(1, stages):
        copy = swap(send0, recv0, 0, stage)
        copy.start()
        copy.wait()
        send0[stage + 1] = send0[stage] + recv0[stage]
    gram = send0[stages]
    g_ref[:half, :] = gram[:, :width]
    g_ref[half:, :half] = gram[:, half:width].T
    g_ref[half:, half:] = gram[:, width:]
    mean_sq = total(pairs_done()) / (width * pairs)

    row_id = lax.broadcasted_iota(jnp.int32, (width, width), 0)
    col_id = lax.broadcasted_iota(jnp.int32, (width, width), 1)
    eye = (row_id == col_id).astype(F32)
    off_tile[...] = jnp.zeros_like(off_tile)
    first_scale, scales = scalings(width)

    def move(r, c):
        return pltpu.make_async_remote_copy(
            src_ref=mov.at[r, at(c)],
            dst_ref=ab.at[r + 1, at(c)],
            send_sem=move_send.at[r, c],
            recv_sem=move_recv.at[r, c],
            device_id={"pair": after},
            device_id_type=MESH,
        )

    def pass_mass(r):
        return pltpu.make_async_remote_copy(
            src_ref=mass_src.at[r],
            dst_ref=mass_in.at[r],
            send_sem=mass_send.at[r],
            recv_sem=mass_recv.at[r],
            device_id={"pair": after},
            device_id_type=MESH,
        )

    @pl.loop(0, ROUNDS)
    def _(r):
        gram = g_ref[...]
        diag = gram * eye
        denom = jnp.sum(diag, axis=1, keepdims=True) + jnp.sum(diag, axis=0, keepdims=True) + mean_sq
        weight = (col_id.astype(F32) - row_id.astype(F32)) * F32(1.0 / (width - 1))
        skew = gram * weight / denom
        square = wide_dot(skew, skew)
        resid = eye - F32(first_scale) * (eye - square)
        inverse = F32(first_scale) * (eye + skew)

        def refine(i, carry):
            resid, inverse = carry
            scale = F32(scales[0])
            for j in range(1, STEPS - 1):
                scale = jnp.where(i == j, F32(scales[j]), scale)
            inverse = scale * (inverse + wide_dot(inverse, resid))
            resid = scale * wide_dot(resid, resid) + (1.0 - scale) * eye
            return resid, inverse

        resid, inverse = lax.fori_loop(0, STEPS - 1, refine, (resid, inverse))
        inverse = F32(scales[STEPS - 1]) * (inverse + wide_dot(inverse, resid))
        wrong = eye - (inverse - full_dot(skew, inverse))
        inverse = inverse + wide_dot(inverse, wrong)
        rotation = 2.0 * inverse - eye
        flag = jnp.full((width, width), plan_ref[r, 0], jnp.int32)
        turned = jnp.concatenate([rotation[:, half:], rotation[:, :half]], axis=1)
        rotation = jnp.where(flag == 1, turned, rotation)
        high, low = split(rotation)
        q_hi[...] = high
        q_lo[...] = low
        q_src[r] = rotation[:, half:]
        pass_q(r).start()

        @pl.loop(0, CHUNKS)
        def _(c):
            high, low = split(jnp.concatenate([kb[r, at(c)], ab[r, at(c)]], axis=1))
            y = dot(high, q_hi[...]) + (dot(high, q_lo[...]) + dot(low, q_hi[...]))
            mov[r, at(c)] = y[:, half:]
            move(r, c).start()
            kb[r + 1, at(c)] = y[:, :half]

        @pl.loop(0, RAW_BLOCKS)
        def _(c):
            high, low = split(jnp.concatenate([kb[r, raw_at(c)], ab[r, raw_at(c)]], axis=1))
            keep_high, keep_low = q_hi[:, :half], q_lo[:, :half]
            kb[r + 1, raw_at(c)] = dot(high, keep_high) + (dot(high, keep_low) + dot(low, keep_high))

        off = gram * (1.0 - eye)
        tile_row = lax.broadcasted_iota(jnp.int32, off_tile.shape, 0)
        off_tile[...] = jnp.where(tile_row == r, total(off * off), off_tile[...])

        def finish_raw():
            pass_raw(r, 0).wait()
            pass_raw(r, 1).wait()
            pass_q(r).wait()

            @pl.loop(0, RAW_BLOCKS)
            def _(c):
                high, low = split(
                    jnp.concatenate([raw_in[r, 0, raw_at(c)], raw_in[r, 1, raw_at(c)]], axis=1)
                )
                move_high, move_low = split(q_in[r])
                ab[r + 1, raw_at(c)] = dot(high, move_high) + (dot(high, move_low) + dot(low, move_high))

        @pl.when(r < ROUNDS - 1)
        def _():
            mass = full_tdot(rotation, full_dot(gram, rotation))
            mass_src[r] = mass[half:, half:]
            pass_mass(r).start()
            g_ref[:half, :half] = mass[:half, :half]
            acc[...] = jnp.zeros_like(acc)
            finish_raw()

            def cross_gram(where):
                k_high, k_low = split(kb[r + 1, where])
                m_high, m_low = split(ab[r + 1, where])
                acc[...] += tdot(k_high, m_high) + (tdot(k_high, m_low) + tdot(k_low, m_high))

            @pl.loop(0, RAW_BLOCKS)
            def _(c):
                cross_gram(raw_at(c))

            pass_raw(r + 1, 0).start()
            pass_raw(r + 1, 1).start()

            @pl.loop(0, CHUNKS)
            def _(c):
                move(r, c).wait()
                cross_gram(at(c))

            sendg[r, 0] = acc[...]
            cross = reduce_rows(sendg.at[r], recvg.at[r], r + 1)
            pass_mass(r).wait()
            g_ref[:half, half:] = cross
            g_ref[half:, :half] = cross.T
            g_ref[half:, half:] = mass_in[r]

        @pl.when(r == ROUNDS - 1)
        def _():
            finish_raw()

    off_done = share("pair", pairs, off_tile, off_pairs, off_send, off_recv)

    @pl.loop(0, CHUNKS)
    def _(c):
        store(c, 0).start()

    store_raw(0).start()
    store_raw(1).start()
    off_ref[...] = jnp.sqrt(off_done() / (pairs * width * (width - 1))) / mean_sq

    @pl.loop(0, CHUNKS)
    def _(c):
        move(ROUNDS - 1, c).wait()
        store(c, 1).start()

    @pl.loop(0, CHUNKS)
    def _(c):
        store(c, 0).wait()
        store(c, 1).wait()

    store_raw(0).wait()
    store_raw(1).wait()


def local(matrix, plan):
    rows, width = matrix.shape
    half = width // 2
    pairs = lax.axis_size("pair")
    groups = lax.axis_size("rows")
    if groups & (groups - 1) or rows % 1024:
        raise ValueError("sizes")
    stages = groups.bit_length() - 1
    raw = rows // 8
    dma = pltpu.SemaphoreType.DMA
    tile = (8, 128)
    rotated, off = pl.pallas_call(
        functools.partial(kernel, pairs, groups),
        out_shape=(
            jax.ShapeDtypeStruct(matrix.shape, F32),
            jax.ShapeDtypeStruct(tile, F32),
        ),
        in_specs=[pl.BlockSpec(memory_space=pl.ANY), pl.BlockSpec(memory_space=pltpu.SMEM)],
        out_specs=(pl.BlockSpec(memory_space=pl.ANY), pl.BlockSpec(memory_space=pltpu.VMEM)),
        scratch_shapes=[
            pltpu.VMEM((ROUNDS + 1, rows, half), F32),
            pltpu.VMEM((ROUNDS + 1, rows, half), F32),
            pltpu.VMEM((ROUNDS, rows, half), F32),
            pltpu.VMEM((width, width), F32),
            pltpu.VMEM((half, half), F32),
            pltpu.VMEM((width, width), BF16),
            pltpu.VMEM((width, width), BF16),
            pltpu.VMEM((stages + 1, half, 3 * half), F32),
            pltpu.VMEM((stages, half, 3 * half), F32),
            pltpu.VMEM((ROUNDS, stages + 1, half, half), F32),
            pltpu.VMEM((ROUNDS, stages, half, half), F32),
            pltpu.VMEM((ROUNDS, half, half), F32),
            pltpu.VMEM((ROUNDS, half, half), F32),
            pltpu.VMEM(tile, F32),
            pltpu.VMEM((groups,) + tile, F32),
            pltpu.VMEM(tile, F32),
            pltpu.VMEM((pairs,) + tile, F32),
            pltpu.VMEM(tile, F32),
            pltpu.VMEM((pairs,) + tile, F32),
            pltpu.VMEM((ROUNDS, 2, raw, half), F32),
            pltpu.VMEM((ROUNDS, width, half), F32),
            pltpu.VMEM((ROUNDS, width, half), F32),
            dma((2, CHUNKS)),
            dma((2, CHUNKS + 1)),
            dma((ROUNDS, CHUNKS)),
            dma((ROUNDS, CHUNKS)),
            dma((ROUNDS, stages)),
            dma((ROUNDS, stages)),
            dma((ROUNDS,)),
            dma((ROUNDS,)),
            dma((groups,)),
            dma((groups,)),
            dma((pairs,)),
            dma((pairs,)),
            dma((pairs,)),
            dma((pairs,)),
            dma((ROUNDS, 2)),
            dma((ROUNDS, 2)),
            dma((ROUNDS,)),
            dma((ROUNDS,)),
        ],
        compiler_params=pltpu.CompilerParams(
            collective_id=0, has_side_effects=True, vmem_limit_bytes=50 * 2**20
        ),
    )(matrix, plan)
    return rotated, off[:ROUNDS, 0]


def solution(mesh):
    in_specs = (P("rows", "pair"), P(None, "pair"))
    out_specs = (P("rows", "pair"), P())
    return jax.shard_map(local, mesh=mesh, in_specs=in_specs, out_specs=out_specs, check_vma=False)
```

```python
import functools

import jax
import jax.numpy as jnp
from jax import lax
from jax.experimental import pallas as pl
from jax.experimental.pallas import tpu as pltpu
from jax.sharding import PartitionSpec as P

ROUNDS = 3
CHUNKS = 8
RAW_BLOCKS = 2
STEPS = 7
MESH = pl.DeviceIdType.MESH
F32 = jnp.float32
BF16 = jnp.bfloat16


def split(x):
    high = x.astype(BF16)
    return high, (x - high.astype(F32)).astype(BF16)


def dot(a, b):
    return jnp.dot(a, b, preferred_element_type=F32)


def tdot(a, b):
    return lax.dot_general(a, b, (((0,), (0,)), ((), ())), preferred_element_type=F32)


def full_dot(a, b):
    return jnp.dot(a, b, precision=lax.Precision.HIGHEST, preferred_element_type=F32)


def wide_dot(a, b):
    a_high, a_low = split(a)
    b_high, b_low = split(b)
    return dot(a_high, b_high) + (dot(a_high, b_low) + dot(a_low, b_high))


def full_tdot(a, b):
    return lax.dot_general(
        a, b, (((0,), (0,)), ((), ())), precision=lax.Precision.HIGHEST, preferred_element_type=F32
    )


def total(x):
    return jnp.sum(jnp.sum(x, axis=1, keepdims=True), axis=0, keepdims=True)


def scalings(width):
    spread = sum((i - j) ** 2 for i in range(width) for j in range(width)) / (width - 1) ** 2
    top = 1.0 + spread / 8.0
    first = 2.0 / (1.0 + top)
    err = (top - 1.0) / (top + 1.0)
    out = []
    for _ in range(STEPS):
        scale = 2.0 / (2.0 - err * err)
        out.append(scale)
        err = scale - 1.0
    return first, out


def share(axis, peers, tile_ref, slots, send_sems, recv_sems):
    me = lax.axis_index(axis)

    def copy_to(step):
        to = lax.rem(me + step, peers)
        return pltpu.make_async_remote_copy(
            src_ref=tile_ref,
            dst_ref=slots.at[me],
            send_sem=send_sems.at[step],
            recv_sem=recv_sems.at[step],
            device_id={axis: to},
            device_id_type=MESH,
        )

    def start(step, carry):
        copy_to(step).start()
        return carry

    def finish(step, carry):
        copy_to(step).wait()
        return carry

    lax.fori_loop(1, peers, start, 0)

    def done():
        lax.fori_loop(1, peers, finish, 0)
        slots[me] = tile_ref[...]

        def add(i, acc):
            return acc + slots[i]

        return lax.fori_loop(0, peers, add, jnp.zeros(tile_ref.shape, F32))

    return done


def kernel(
    pairs, groups, x_ref, plan_ref, out_ref, off_ref,
    kb, ab, mov, g_ref, acc, q_hi, q_lo, send0, recv0, sendg, recvg, mass_src, mass_in,
    sq_src, sq_rows, sq_tile, sq_pairs, off_tile, off_pairs, raw_in, q_src, q_in,
    load_sem, store_sem, move_send, move_recv, ex_send, ex_recv, mass_send, mass_recv,
    sqr_send, sqr_recv, sqp_send, sqp_recv, off_send, off_recv,
    raw_send, raw_recv, q_send, q_recv,
):
    rows_all, width = x_ref.shape
    half = width // 2
    raw = raw_in.shape[2]
    rows = (rows_all - raw) // CHUNKS
    load_rows = rows_all // CHUNKS
    raw_rows = raw // RAW_BLOCKS
    stages = groups.bit_length() - 1
    pair = lax.axis_index("pair")
    group = lax.axis_index("rows")
    after = lax.rem(pair + 1, pairs)

    def at(c):
        return pl.ds(pl.multiple_of(raw + c * rows, 16), rows)

    def load_at(c):
        return pl.ds(pl.multiple_of(c * load_rows, load_rows), load_rows)

    def raw_at(c):
        return pl.ds(pl.multiple_of(c * raw_rows, raw_rows), raw_rows)

    def load(c, side):
        dst = ab if side else kb
        return pltpu.make_async_copy(
            x_ref.at[load_at(c), pl.ds(side * half, half)], dst.at[0, load_at(c)], load_sem.at[side, c]
        )

    def store(c, side):
        src = ab if side else kb
        return pltpu.make_async_copy(
            src.at[ROUNDS, at(c)], out_ref.at[at(c), pl.ds(side * half, half)], store_sem.at[side, c]
        )

    def store_raw(side):
        src = ab if side else kb
        where = pl.ds(0, raw)
        return pltpu.make_async_copy(
            src.at[ROUNDS, where], out_ref.at[where, pl.ds(side * half, half)], store_sem.at[side, CHUNKS]
        )

    def pass_raw(r, side):
        src = ab if side else kb
        return pltpu.make_async_remote_copy(
            src_ref=src.at[r, pl.ds(0, raw)],
            dst_ref=raw_in.at[r, side],
            send_sem=raw_send.at[r, side],
            recv_sem=raw_recv.at[r, side],
            device_id={"pair": after},
            device_id_type=MESH,
        )

    def pass_q(r):
        return pltpu.make_async_remote_copy(
            src_ref=q_src.at[r],
            dst_ref=q_in.at[r],
            send_sem=q_send.at[r],
            recv_sem=q_recv.at[r],
            device_id={"pair": after},
            device_id_type=MESH,
        )

    @pl.loop(0, CHUNKS)
    def _(c):
        load(c, 0).start()
        load(c, 1).start()

    barrier = pltpu.get_barrier_semaphore()

    @pl.loop(1, pairs)
    def _(step):
        pl.semaphore_signal(
            barrier, inc=1, device_id={"pair": lax.rem(pair + step, pairs)}, device_id_type=MESH
        )

    @pl.loop(1, groups)
    def _(step):
        pl.semaphore_signal(
            barrier, inc=1, device_id={"rows": lax.rem(group + step, groups)}, device_id_type=MESH
        )

    sq_src[...] = jnp.zeros_like(sq_src)

    @pl.loop(0, CHUNKS)
    def _(c):
        load(c, 0).wait()
        load(c, 1).wait()
        k = kb[0, load_at(c)]
        m = ab[0, load_at(c)]
        sq_src[...] += jnp.sum((k * k + m * m).reshape(load_rows // 8, 8, half), axis=0)

    pl.semaphore_wait(barrier, pairs - 1 + groups - 1)
    pass_raw(0, 0).start()
    pass_raw(0, 1).start()
    rows_done = share("rows", groups, sq_src, sq_rows, sqr_send, sqr_recv)

    g_ref[...] = jnp.zeros_like(g_ref)
    mass_low = jnp.zeros((width, width), F32)

    def first_gram(c, carry):
        high_high, high_low = carry
        high, low = split(jnp.concatenate([kb[0, load_at(c)], ab[0, load_at(c)]], axis=1))
        return high_high + tdot(high, high), high_low + tdot(high, low)

    high_high, high_low = lax.fori_loop(0, CHUNKS, first_gram, (mass_low, mass_low))
    gram = high_high + high_low + high_low.T
    send0[0] = jnp.concatenate([gram[:half], gram[half:, half:]], axis=1)

    def swap(send, recv, step, stage):
        return pltpu.make_async_remote_copy(
            src_ref=send.at[stage],
            dst_ref=recv.at[stage],
            send_sem=ex_send.at[step, stage],
            recv_sem=ex_recv.at[step, stage],
            device_id={"rows": jnp.bitwise_xor(group, 1 << stage)},
            device_id_type=MESH,
        )

    def reduce_rows(send, recv, step):
        for stage in range(stages):
            copy = swap(send, recv, step, stage)
            copy.start()
            copy.wait()
            send[stage + 1] = send[stage] + recv[stage]
        return send[stages]

    first_swap = swap(send0, recv0, 0, 0)
    first_swap.start()
    sq_tile[...] = rows_done()
    pairs_done = share("pair", pairs, sq_tile, sq_pairs, sqp_send, sqp_recv)
    first_swap.wait()
    send0[1] = send0[0] + recv0[0]
    for stage in range(1, stages):
        copy = swap(send0, recv0, 0, stage)
        copy.start()
        copy.wait()
        send0[stage + 1] = send0[stage] + recv0[stage]
    gram = send0[stages]
    g_ref[:half, :] = gram[:, :width]
    g_ref[half:, :half] = gram[:, half:width].T
    g_ref[half:, half:] = gram[:, width:]
    mean_sq = total(pairs_done()) / (width * pairs)

    row_id = lax.broadcasted_iota(jnp.int32, (width, width), 0)
    col_id = lax.broadcasted_iota(jnp.int32, (width, width), 1)
    eye = (row_id == col_id).astype(F32)
    off_tile[...] = jnp.zeros_like(off_tile)
    first_scale, scales = scalings(width)

    def move(r, c):
        return pltpu.make_async_remote_copy(
            src_ref=mov.at[r, at(c)],
            dst_ref=ab.at[r + 1, at(c)],
            send_sem=move_send.at[r, c],
            recv_sem=move_recv.at[r, c],
            device_id={"pair": after},
            device_id_type=MESH,
        )

    def pass_mass(r):
        return pltpu.make_async_remote_copy(
            src_ref=mass_src.at[r],
            dst_ref=mass_in.at[r],
            send_sem=mass_send.at[r],
            recv_sem=mass_recv.at[r],
            device_id={"pair": after},
            device_id_type=MESH,
        )

    @pl.loop(0, ROUNDS)
    def _(r):
        gram = g_ref[...]
        diag = gram * eye
        denom = jnp.sum(diag, axis=1, keepdims=True) + jnp.sum(diag, axis=0, keepdims=True) + mean_sq
        weight = (col_id.astype(F32) - row_id.astype(F32)) * F32(1.0 / (width - 1))
        skew = gram * weight / denom
        square = wide_dot(skew, skew)
        resid = eye - F32(first_scale) * (eye - square)
        inverse = F32(first_scale) * (eye + skew)

        def refine(i, carry):
            resid, inverse = carry
            scale = F32(scales[0])
            for j in range(1, STEPS - 1):
                scale = jnp.where(i == j, F32(scales[j]), scale)
            inverse = scale * (inverse + wide_dot(inverse, resid))
            resid = scale * wide_dot(resid, resid) + (1.0 - scale) * eye
            return resid, inverse

        resid, inverse = lax.fori_loop(0, STEPS - 1, refine, (resid, inverse))
        inverse = F32(scales[STEPS - 1]) * (inverse + wide_dot(inverse, resid))
        wrong = eye - (inverse - full_dot(skew, inverse))
        inverse = inverse + wide_dot(inverse, wrong)
        rotation = 2.0 * inverse - eye
        flag = jnp.full((width, width), plan_ref[r, 0], jnp.int32)
        turned = jnp.concatenate([rotation[:, half:], rotation[:, :half]], axis=1)
        rotation = jnp.where(flag == 1, turned, rotation)
        high, low = split(rotation)
        q_hi[...] = high
        q_lo[...] = low
        q_src[r] = rotation[:, half:]
        pass_q(r).start()

        @pl.loop(0, CHUNKS)
        def _(c):
            high, low = split(jnp.concatenate([kb[r, at(c)], ab[r, at(c)]], axis=1))
            y = dot(high, q_hi[...]) + (dot(high, q_lo[...]) + dot(low, q_hi[...]))
            mov[r, at(c)] = y[:, half:]
            move(r, c).start()
            kb[r + 1, at(c)] = y[:, :half]

        @pl.loop(0, RAW_BLOCKS)
        def _(c):
            high, low = split(jnp.concatenate([kb[r, raw_at(c)], ab[r, raw_at(c)]], axis=1))
            keep_high, keep_low = q_hi[:, :half], q_lo[:, :half]
            kb[r + 1, raw_at(c)] = dot(high, keep_high) + (dot(high, keep_low) + dot(low, keep_high))

        off = gram * (1.0 - eye)
        tile_row = lax.broadcasted_iota(jnp.int32, off_tile.shape, 0)
        off_tile[...] = jnp.where(tile_row == r, total(off * off), off_tile[...])

        def finish_raw():
            pass_raw(r, 0).wait()
            pass_raw(r, 1).wait()
            pass_q(r).wait()

            @pl.loop(0, RAW_BLOCKS)
            def _(c):
                high, low = split(
                    jnp.concatenate([raw_in[r, 0, raw_at(c)], raw_in[r, 1, raw_at(c)]], axis=1)
                )
                move_high, move_low = split(q_in[r])
                ab[r + 1, raw_at(c)] = dot(high, move_high) + (dot(high, move_low) + dot(low, move_high))

        @pl.when(r < ROUNDS - 1)
        def _():
            mass = full_tdot(rotation, full_dot(gram, rotation))
            mass_src[r] = mass[half:, half:]
            pass_mass(r).start()
            g_ref[:half, :half] = mass[:half, :half]
            acc[...] = jnp.zeros_like(acc)
            finish_raw()

            def cross_gram(where):
                k_high, k_low = split(kb[r + 1, where])
                m_high, m_low = split(ab[r + 1, where])
                acc[...] += tdot(k_high, m_high) + (tdot(k_high, m_low) + tdot(k_low, m_high))

            @pl.loop(0, RAW_BLOCKS)
            def _(c):
                cross_gram(raw_at(c))

            pass_raw(r + 1, 0).start()
            pass_raw(r + 1, 1).start()

            @pl.loop(0, CHUNKS)
            def _(c):
                move(r, c).wait()
                cross_gram(at(c))

            sendg[r, 0] = acc[...]
            cross = reduce_rows(sendg.at[r], recvg.at[r], r + 1)
            pass_mass(r).wait()
            g_ref[:half, half:] = cross
            g_ref[half:, :half] = cross.T
            g_ref[half:, half:] = mass_in[r]

        @pl.when(r == ROUNDS - 1)
        def _():
            finish_raw()

    off_done = share("pair", pairs, off_tile, off_pairs, off_send, off_recv)

    @pl.loop(0, CHUNKS)
    def _(c):
        store(c, 0).start()

    store_raw(0).start()
    store_raw(1).start()
    off_ref[...] = jnp.sqrt(off_done() / (pairs * width * (width - 1))) / mean_sq

    @pl.loop(0, CHUNKS)
    def _(c):
        move(ROUNDS - 1, c).wait()
        store(c, 1).start()

    @pl.loop(0, CHUNKS)
    def _(c):
        store(c, 0).wait()
        store(c, 1).wait()

    store_raw(0).wait()
    store_raw(1).wait()


def local(matrix, plan):
    rows, width = matrix.shape
    half = width // 2
    pairs = lax.axis_size("pair")
    groups = lax.axis_size("rows")
    if groups & (groups - 1) or rows % 1024:
        raise ValueError("sizes")
    stages = groups.bit_length() - 1
    raw = rows // 8
    dma = pltpu.SemaphoreType.DMA
    tile = (8, 128)
    rotated, off = pl.pallas_call(
        functools.partial(kernel, pairs, groups),
        out_shape=(
            jax.ShapeDtypeStruct(matrix.shape, F32),
            jax.ShapeDtypeStruct(tile, F32),
        ),
        in_specs=[pl.BlockSpec(memory_space=pl.ANY), pl.BlockSpec(memory_space=pltpu.SMEM)],
        out_specs=(pl.BlockSpec(memory_space=pl.ANY), pl.BlockSpec(memory_space=pltpu.VMEM)),
        scratch_shapes=[
            pltpu.VMEM((ROUNDS + 1, rows, half), F32),
            pltpu.VMEM((ROUNDS + 1, rows, half), F32),
            pltpu.VMEM((ROUNDS, rows, half), F32),
            pltpu.VMEM((width, width), F32),
            pltpu.VMEM((half, half), F32),
            pltpu.VMEM((width, width), BF16),
            pltpu.VMEM((width, width), BF16),
            pltpu.VMEM((stages + 1, half, 3 * half), F32),
            pltpu.VMEM((stages, half, 3 * half), F32),
            pltpu.VMEM((ROUNDS, stages + 1, half, half), F32),
            pltpu.VMEM((ROUNDS, stages, half, half), F32),
            pltpu.VMEM((ROUNDS, half, half), F32),
            pltpu.VMEM((ROUNDS, half, half), F32),
            pltpu.VMEM(tile, F32),
            pltpu.VMEM((groups,) + tile, F32),
            pltpu.VMEM(tile, F32),
            pltpu.VMEM((pairs,) + tile, F32),
            pltpu.VMEM(tile, F32),
            pltpu.VMEM((pairs,) + tile, F32),
            pltpu.VMEM((ROUNDS, 2, raw, half), F32),
            pltpu.VMEM((ROUNDS, width, half), F32),
            pltpu.VMEM((ROUNDS, width, half), F32),
            dma((2, CHUNKS)),
            dma((2, CHUNKS + 1)),
            dma((ROUNDS, CHUNKS)),
            dma((ROUNDS, CHUNKS)),
            dma((ROUNDS, stages)),
            dma((ROUNDS, stages)),
            dma((ROUNDS,)),
            dma((ROUNDS,)),
            dma((groups,)),
            dma((groups,)),
            dma((pairs,)),
            dma((pairs,)),
            dma((pairs,)),
            dma((pairs,)),
            dma((ROUNDS, 2)),
            dma((ROUNDS, 2)),
            dma((ROUNDS,)),
            dma((ROUNDS,)),
        ],
        compiler_params=pltpu.CompilerParams(
            collective_id=0, has_side_effects=True, vmem_limit_bytes=34 * 2**20
        ),
    )(matrix, plan)
    return rotated, off[:ROUNDS, 0]


def solution(mesh):
    in_specs = (P("rows", "pair"), P(None, "pair"))
    out_specs = (P("rows", "pair"), P())
    return jax.shard_map(local, mesh=mesh, in_specs=in_specs, out_specs=out_specs, check_vma=False)
```
